32 devices in a mesh: tx: 4 (over x, core), py: 2 (over y), pz: 4 (over z).
Axes of the slice: x: 2, y: 2, z: 4, core: 2. Of those that a mesh axis runs over, the one named last changes fastest.
Arguments:
- fields: float32 [16, 2, 128, 128, 128], P('tx', None, 'py', 'pz'), may hold values from 0.5 to 1.5
- sources: float32 [16, 2, 128, 128, 128], P('tx', None, 'py', 'pz'), may hold values from -12 to 12
- green: float32 [2, 128, 128, 128], P(None, 'pz', 'py'), may hold values from -6 to 6
Outputs:
- contrast_fine: float32 [2, 256, 256, 256], P(None, 'py', 'pz')
- scattered: float32 [4, 2, 256, 256, 256], P('tx', None, 'py', 'pz')
The draws below stay inside these ranges and needn't reach their ends.
All inputs are finite; a program needn't handle non-finite values.
Results may differ from the reference program's by a relative error of at most 0.00014.
Values sent between devices are 32-bit elements; how exact they have to be, the bound alone decides.
A program may use at most 192 MiB of HBM per device.

```python
import jax
import jax.numpy as jnp
from jax import lax

COARSE = 128
FINE = 256
PART_DEV = 4
TRANSMITTERS = 16


def levels(key, dims, pieces, least, largest):
    def one(axis_at, blocks):
        steps = jax.random.uniform(jax.random.fold_in(jax.random.fold_in(key, 6), axis_at), (blocks,), jnp.float32, least / len(pieces), largest / len(pieces))
        return jnp.repeat(jnp.exp(steps), dims[axis_at] // blocks).reshape((-1,) + (1,) * (len(dims) - axis_at - 1))

    level = one(*pieces[0])
    for cut in pieces[1:]:
        level = level * one(*cut)
    return level


def bell_draw(key, dims, deviation, limit, split=(), held_as=jnp.bfloat16):
    level = levels(key, dims, split, -0.22, 0.18) if split else 1.0
    array = jax.random.normal(key, dims, jnp.float32) * deviation * level
    return jnp.minimum(jnp.maximum(array, -limit), limit).astype(held_as)


def setup_inputs(seed: int = 0) -> dict:
    arg_keys = jax.random.split(jax.random.key(seed), 4)
    return {
        "fields": jnp.clip(0.5 + 1.0 * jax.random.uniform(arg_keys[0], (TRANSMITTERS, 2, COARSE, COARSE, COARSE), jnp.float32) ** levels(arg_keys[0], (TRANSMITTERS, 2, COARSE, COARSE, COARSE), ((0, 4), (2, 2), (3, 4)), -0.2, 0.2), 0.5, 1.5),
        "sources": bell_draw(arg_keys[1], (TRANSMITTERS, 2, COARSE, COARSE, COARSE), 2.0, 12.0, ((0, 4), (2, 2), (3, 4)), jnp.float32),
        "green": bell_draw(arg_keys[2], (2, COARSE, COARSE, COARSE), 1.0, 6.0, ((1, 4), (2, 2)), jnp.float32),
    }


def placed_indices():
    indices = jnp.arange(COARSE, dtype=jnp.int32)
    return jnp.where(indices < COARSE // 2, indices, indices - COARSE + FINE).astype(jnp.int32)


def place_fine(values):
    placed = placed_indices()
    padded = jnp.zeros((FINE, FINE, FINE), values.dtype)
    return padded.at[placed[:, None, None], placed[None, :, None], placed[None, None, :]].set(values)


def prolong(coarse_field):
    spectrum = jnp.fft.fftn(coarse_field)
    return jnp.fft.ifftn(place_fine(spectrum)) * ((FINE / COARSE) ** 3)


def reference(fields, sources, green):
    field_real = fields[:, 0]
    field_imag = fields[:, 1]
    source_real = sources[:, 0]
    source_imag = sources[:, 1]
    numer_real = jnp.sum(source_real * field_real + source_imag * field_imag, axis=0)
    numer_imag = jnp.sum(source_imag * field_real - source_real * field_imag, axis=0)
    denominator = jnp.sum(field_real * field_real + field_imag * field_imag, axis=0)
    contrast = (numer_real / denominator) + 1j * (numer_imag / denominator)
    contrast_fine = prolong(contrast)
    green_spectrum = place_fine(jnp.transpose(green[0] + 1j * green[1], (2, 1, 0)))

    def scatter_one(source_one):
        fine_source = prolong(source_one[0] + 1j * source_one[1])
        domain_field = jnp.fft.ifftn(green_spectrum * jnp.fft.fftn(fine_source))
        product = contrast_fine * domain_field
        return jnp.stack([jnp.real(product), jnp.imag(product)]).astype(jnp.float32)

    scattered = lax.map(scatter_one, sources[::PART_DEV])
    fine_parts = jnp.stack([jnp.real(contrast_fine), jnp.imag(contrast_fine)]).astype(jnp.float32)
    return fine_parts, scattered
```

```python
import functools
import math

import jax
import jax.numpy as jnp
import ml_dtypes
import numpy as np
from jax import lax
from jax.experimental import pallas as pl
from jax.experimental.pallas import tpu as pltpu
from jax.sharding import PartitionSpec as P

F32 = jnp.float32
BF16 = jnp.bfloat16
NN = (((1,), (0,)), ((), ()))
NT = (((1,), (1,)), ((), ()))


def signed(count):
    index = np.arange(count)
    return np.where(index < count // 2, index, index - count)


def forward_matrix(coarse):
    index = np.arange(coarse)
    return np.exp(-2j * np.pi * ((index[:, None] * index[None, :]) % coarse) / coarse)


def inverse_matrix(coarse, fine):
    phases = (np.arange(fine)[:, None] * signed(coarse)[None, :]) % fine
    return np.exp(2j * np.pi * phases / fine) / coarse


def halves(matrix):
    high = matrix.astype(ml_dtypes.bfloat16)
    low = (matrix - high.astype(np.float64)).astype(ml_dtypes.bfloat16)
    return np.stack([high, low], axis=-3)


def block_form(matrix):
    re, im = matrix.real, matrix.imag
    return np.stack([np.stack([re, -im], 1), np.stack([im, re], 1)], 0)


def split(x):
    high = x.astype(BF16)
    return high, (x - high.astype(F32)).astype(BF16)


def product_left(m_ref, x, dims):
    high, low = split(x)
    mh, ml = m_ref[0], m_ref[1]
    dot = functools.partial(lax.dot_general, dimension_numbers=dims, preferred_element_type=F32)
    return dot(mh, high) + dot(mh, low) + dot(ml, high)


def product_right(x, m_ref):
    high, low = split(x)
    mh, ml = m_ref[0], m_ref[1]
    dot = functools.partial(lax.dot_general, dimension_numbers=NN, preferred_element_type=F32)
    return dot(high, mh) + dot(low, mh) + dot(high, ml)


def times_i(x):
    half = x.shape[1] // 2
    return jnp.concatenate([-x[:, half:], x[:, :half]], axis=1)


def depth_forward(m_ref, x_ref, o_ref):
    parts, _, rows, _ = o_ref.shape
    for s in range(x_ref.shape[3]):
        re, im = x_ref[0, 0, :, s, :], x_ref[0, 1, :, s, :]
        both = jnp.concatenate(
            [jnp.concatenate([re, -im], axis=1), jnp.concatenate([im, re], axis=1)], axis=0
        )
        out = product_left(m_ref, both, NT)
        for p in range(parts):
            o_ref[p, s] = out[p * rows : (p + 1) * rows]


def middle_forward(m_ref, x_ref, o_ref):
    parts, _, rows, lanes = o_ref.shape
    for s in range(x_ref.shape[2]):
        x = x_ref[:, :, s, :].reshape(-1, lanes)
        out = product_left(m_ref, jnp.concatenate([x, times_i(x)], axis=0), NN)
        for p in range(parts):
            o_ref[p, s] = out[p * rows : (p + 1) * rows]


def top_forward(m_ref, x_ref, g_ref, o_ref):
    parts, count, rows, lanes = x_ref.shape
    x = jnp.concatenate([x_ref[p].reshape(count * rows, lanes) for p in range(parts)], axis=1)
    v = product_right(x, m_ref)
    coarse = v.shape[1] // 2
    vr, vi = v[:, :coarse], v[:, coarse:]
    gr, gi = g_ref[0].reshape(count * rows, coarse), g_ref[1].reshape(count * rows, coarse)
    wr = vr * gr - vi * gi
    wi = vr * gi + vi * gr
    wide = coarse // parts
    for p in range(parts):
        cut = slice(p * wide, (p + 1) * wide)
        o_ref[p] = jnp.concatenate([wr[:, cut], wi[:, cut]], axis=1).reshape(count, rows, lanes)


def middle_inverse(m_ref, x_ref, *o_refs):
    parts, _, rows, lanes = o_refs[0].shape
    for s in range(x_ref.shape[1]):
        x = jnp.concatenate([x_ref[p, s] for p in range(x_ref.shape[0])], axis=0)
        out = product_left(m_ref, jnp.concatenate([x, times_i(x)], axis=0), NN)
        for p in range(parts):
            for h, o_ref in enumerate(o_refs):
                at = (p * len(o_refs) + h) * rows
                o_ref[p, s] = out[at : at + rows]


def middle_refine(m_ref, x_ref, o_ref):
    rows = o_ref.shape[2]
    for i in range(x_ref.shape[2]):
        pieces = [x_ref[q, c, i] for q in range(x_ref.shape[0]) for c in range(2)]
        out = product_left(m_ref, jnp.concatenate(pieces, axis=0), NN)
        o_ref[0, i] = out[:rows]
        o_ref[1, i] = out[rows:]


def last_product(t, m_ref):
    top = t.shape[0] // 2
    out = product_right(jnp.concatenate([t[:top], t[top:]], axis=1), m_ref)
    fine = out.shape[1] // 2
    return out[:, :fine], out[:, fine:]


def contrast_last(m1_ref, m3_ref, *refs):
    *x_refs, o_ref = refs
    lanes = x_refs[0].shape[3]
    for s in range(o_ref.shape[2]):
        x = jnp.concatenate([r[:, :, s, :].reshape(-1, lanes) for r in x_refs], axis=0)
        re, im = last_product(product_left(m1_ref, x, NN), m3_ref)
        o_ref[0, :, s, :] = re
        o_ref[1, :, s, :] = im


def scatter_last(slots, m1_ref, m3_ref, c_ref, *refs):
    x_refs, o_ref = refs[:slots], refs[-1]
    lanes = x_refs[0].shape[3]
    for s in range(o_ref.shape[3]):
        x = jnp.concatenate([r[:, :, s, :].reshape(-1, lanes) for r in x_refs], axis=1)
        re, im = last_product(product_left(m1_ref, x, NT), m3_ref)
        cr, ci = c_ref[0, :, s, :], c_ref[1, :, s, :]
        o_ref[0, 0, :, s, :] = cr * re - ci * im
        o_ref[0, 1, :, s, :] = cr * im + ci * re


def whole(array):
    zeros = (0,) * array.ndim
    return pl.BlockSpec(array.shape, lambda i: zeros)


def along(shape, axis, block, offset=0):
    sizes = tuple(block if a == axis else n for a, n in enumerate(shape))
    return pl.BlockSpec(sizes, lambda i: tuple(i + offset if a == axis else 0 for a in range(len(shape))))


def call(body, steps, in_specs, operands, shapes, out_specs, name, flops, aliases=None):
    moved = sum(math.prod(s.shape) * 4 for s in shapes) * 2
    return pl.pallas_call(
        body,
        grid=(steps,),
        in_specs=in_specs,
        out_specs=out_specs,
        out_shape=shapes,
        input_output_aliases=aliases or {},
        name=name,
        cost_estimate=pl.CostEstimate(flops=flops, bytes_accessed=moved, transcendentals=0),
        compiler_params=pltpu.CompilerParams(vmem_limit_bytes=56 * 2**20),
    )(*operands)


ROWS = 8


def shape_of(*dims):
    return jax.ShapeDtypeStruct(dims, F32)


def exchange(x, axis):
    return lax.all_to_all(x, axis, 0, 0, tiled=True)


def swap(x, axis, size, bit):
    return lax.ppermute(x, axis, [(i, i ^ bit) for i in range(size)])


def gather_slots(pieces, axis, size):
    bit = size // 2
    order = [(0, p) for p in pieces]
    while bit:
        order = order + [(j | bit, swap(p, axis, size, bit)) for j, p in order]
        bit //= 2
    return order


def aligned_device(tx, py, pz, chunks, fields, sources, green):
    coarse = fields.shape[4]
    fine = 2 * coarse
    x1, x2 = fields.shape[2], fields.shape[3]
    f1, f2 = fine // py, fine // pz
    lanes = 2 * x1
    part = x1 // tx
    k3 = coarse // pz
    me_y, me_z, me_x = lax.axis_index("py"), lax.axis_index("pz"), lax.axis_index("tx")

    fwd, inv = forward_matrix(coarse), inverse_matrix(coarse, fine)
    refine = inv @ fwd
    ri = lambda m: np.concatenate([m.real, m.imag], axis=1)
    m_fwd = jnp.asarray(halves(ri(fwd)))
    m_inv = jnp.asarray(halves(ri(inv)))
    top = block_form(fwd).reshape(2 * coarse, 2, py, x1).transpose(2, 1, 3, 0)
    m_top = jnp.asarray(halves(top.reshape(2 * coarse, 2 * coarse)))
    last = block_form(inv).transpose(2, 3, 0, 1).reshape(2 * coarse, 2 * fine)
    m_last = jnp.asarray(halves(last))
    last_c = block_form(refine).transpose(2, 3, 0, 1).reshape(2 * coarse, 2 * fine)
    m_last_c = jnp.asarray(halves(last_c))
    first = block_form(inv).reshape(2, py, f1, 2, py, x1)
    m_first = jnp.asarray(
        halves(
            np.stack(
                [
                    first[:, y][:, :, :, [y ^ j for j in range(py)]].transpose(0, 1, 3, 2, 4)
                    .reshape(2 * f1, 2 * coarse)
                    for y in range(py)
                ]
            )
        )
    )[me_y]
    mid = block_form(refine).reshape(2, pz, f2, 2, pz, x2).transpose(1, 0, 2, 4, 3, 5)
    m_mid = jnp.asarray(halves(mid.reshape(pz, 2 * f2, 2 * coarse)))[me_z]

    fr, fi, sr, si = fields[:, 0], fields[:, 1], sources[:, 0], sources[:, 1]
    numer_re = jnp.sum(sr * fr + si * fi, axis=0)
    numer_im = jnp.sum(si * fr - sr * fi, axis=0)
    denom = jnp.sum(fr * fr + fi * fi, axis=0)
    cut = lambda v: v.reshape(tx, part, x2, coarse)
    sums = exchange(jnp.stack([cut(numer_re), cut(numer_im), cut(denom)], axis=1), "tx")
    sums = jnp.sum(sums, axis=0)
    contrast = sums[:2] / sums[2:]

    spec = call(
        depth_forward, x2 // ROWS,
        [whole(m_fwd), pl.BlockSpec((1, 2, x1, ROWS, coarse), lambda i: (0, 0, 0, i, 0))],
        (m_fwd, sources), [shape_of(pz, x2, k3, lanes)], [along((pz, x2, k3, lanes), 1, ROWS)],
        "depth_forward", 6 * 2 * x2 * coarse * coarse * lanes,
    )[0]
    spec = exchange(spec, "pz")
    spec = call(
        middle_forward, k3 // ROWS,
        [whole(m_fwd), along(spec.shape, 2, ROWS)],
        (m_fwd, spec), [shape_of(py, k3, x1, lanes)], [along((py, k3, x1, lanes), 1, ROWS)],
        "middle_forward", 6 * 2 * k3 * coarse * coarse * lanes,
    )[0]
    spec = exchange(spec, "py")
    spec = call(
        top_forward, k3 // ROWS,
        [whole(m_top), along(spec.shape, 1, ROWS), along(green.shape, 1, ROWS)],
        (m_top, spec, green), [shape_of(py, k3, x1, lanes)], [along((py, k3, x1, lanes), 1, ROWS)],
        "top_forward", 6 * 4 * k3 * x1 * coarse * coarse,
    )[0]
    spec = exchange(spec, "py")

    some = f2 // chunks
    dims = (pz, k3, some, lanes)
    pieces = call(
        middle_inverse, k3 // ROWS,
        [whole(m_inv), along(spec.shape, 1, ROWS)],
        (m_inv, spec), [shape_of(*dims)] * chunks, [along(dims, 1, ROWS)] * chunks,
        "middle_inverse", 6 * 2 * k3 * fine * coarse * lanes,
    )

    spread = jnp.broadcast_to(contrast[None], (pz,) + contrast.shape)
    seen = exchange(spread, "pz")
    ref_dims = (2, part, f2, coarse)
    step = min(4, part)
    mine = call(
        middle_refine, part // step,
        [whole(m_mid), along(seen.shape, 2, step)],
        (m_mid, seen), [shape_of(*ref_dims)], [along(ref_dims, 1, step)],
        "middle_refine", 6 * 4 * part * f2 * coarse * coarse,
    )[0]
    slots = []
    for j, piece in gather_slots([mine], "py", py):
        slots += [(j, piece)]
    order, parts = [s[0] for s in slots], [s[1] for s in slots]
    bit, codes = tx // 2, [(j, 0) for j in order]
    while bit:
        parts = parts + [swap(p, "tx", tx, bit) for p in parts]
        codes = codes + [(j, t | bit) for j, t in codes]
        bit //= 2
    dim1 = block_form(refine).reshape(2, py, f1, 2, py, tx, part)
    table = np.stack(
        [
            np.stack(
                [dim1[:, y][:, :, :, y ^ j, t ^ k] for j, k in codes], axis=2
            ).reshape(2 * f1, 2 * coarse)
            for y in range(py)
            for t in range(tx)
        ]
    )
    m_first_c = jnp.asarray(halves(table))[me_y * tx + me_x]
    out_dims = (2, f1, f2, fine)
    contrast_fine = call(
        contrast_last, f2 // ROWS,
        [whole(m_first_c), whole(m_last_c)] + [along(ref_dims, 2, ROWS)] * len(parts),
        (m_first_c, m_last_c, *parts), [shape_of(*out_dims)], [along(out_dims, 2, ROWS)],
        "contrast_last", 6 * 8 * f1 * f2 * coarse * fine,
    )[0]

    scattered = None
    scat_dims = (1,) + out_dims
    for h, piece in enumerate(pieces):
        piece = exchange(piece, "pz")
        arrived = [p for _, p in gather_slots([piece], "py", py)]
        offset = h * some // ROWS
        specs = [whole(m_first), whole(m_last), along(out_dims, 2, ROWS, offset)]
        specs += [along(dims, 2, ROWS)] * py
        operands = (m_first, m_last, contrast_fine, *arrived)
        aliases = None
        if scattered is not None:
            aliases = {len(operands): 0}
            specs += [pl.BlockSpec(memory_space=pl.ANY)]
            operands += (scattered,)
        scattered = call(
            functools.partial(scatter_last, py), some // ROWS, specs, operands,
            [shape_of(*scat_dims)], [along(scat_dims, 3, ROWS, offset)],
            "scatter_last", 6 * 8 * f1 * some * coarse * fine, aliases,
        )[0]
    return contrast_fine, scattered


def fourier_matrix(out_index, in_index, period, exponent_sign, weight):
    phases = out_index[:, None] * in_index[None, :] % period
    angles = exponent_sign * 2.0 * math.pi / period * phases.astype(jnp.float32)
    cosine = weight * jnp.cos(angles)
    sine_part = weight * jnp.sin(angles)
    return jnp.stack([jnp.stack([cosine, -sine_part], 1), jnp.stack([sine_part, cosine], 1)], 0)


def local_step(values, matrix):
    return jnp.einsum("fcxyl,dkcl->fdyxk", values, matrix, precision=lax.Precision.HIGHEST)


def remote_step(values, matrix):
    return jnp.einsum("fclxy,dkcl->fdxyk", values, matrix, precision=lax.Precision.HIGHEST)


def turn(values, matrix, axis):
    return remote_step(lax.all_to_all(values, axis, split_axis=4, concat_axis=2, tiled=True), matrix)


def forward_pass(values, matrix):
    return turn(turn(local_step(values, matrix), matrix, "pz"), matrix, "py")


def inverse_pass(values, matrix):
    return turn(turn(local_step(values, matrix), matrix, "py"), matrix, "pz")


def complex_product(first_factor, second_factor):
    real_part = first_factor[0] * second_factor[0] - first_factor[1] * second_factor[1]
    imag_part = first_factor[0] * second_factor[1] + first_factor[1] * second_factor[0]
    return jnp.stack([real_part, imag_part])


def general_device(fields, sources, green):
    coarse = fields.shape[4]
    fine = 2 * coarse
    index = jnp.arange(coarse, dtype=jnp.int32)
    fine_index = jnp.arange(fine, dtype=jnp.int32)
    signed_coarse = jnp.where(index < coarse // 2, index, index - coarse)
    unit_coarse = jnp.ones((coarse, 1), F32)
    unit_fine = jnp.ones((fine, 1), F32)
    coarse_forward = fourier_matrix(index, index, coarse, -1.0, unit_coarse)
    padded_inverse = fourier_matrix(fine_index, signed_coarse, fine, 1.0, unit_fine / coarse)
    fr, fi, sr, si = fields[:, 0], fields[:, 1], sources[:, 0], sources[:, 1]
    numer_re = jnp.sum(sr * fr + si * fi, axis=0)
    numer_im = jnp.sum(si * fr - sr * fi, axis=0)
    denom = jnp.sum(fr * fr + fi * fi, axis=0)
    numer_re, numer_im, denom = lax.psum((numer_re, numer_im, denom), "tx")
    contrast = jnp.stack([numer_re / denom, numer_im / denom])[None]
    contrast_fine = inverse_pass(forward_pass(contrast, coarse_forward), padded_inverse)[0]
    spectrum = forward_pass(sources[0:1], coarse_forward)
    weighted = complex_product(spectrum[0], green)[None]
    domain_field = inverse_pass(weighted, padded_inverse)[0]
    return contrast_fine, complex_product(contrast_fine, domain_field)[None]


def power_of_two(n):
    return n & (n - 1) == 0


def solution(mesh):
    tx, py, pz = mesh.shape["tx"], mesh.shape["py"], mesh.shape["pz"]
    chunks = 2

    def on_device(fields, sources, green):
        x1, x2, coarse = fields.shape[2:]
        fine_block = 2 * coarse // pz
        aligned = (
            power_of_two(tx) and power_of_two(py) and coarse % 128 == 0
            and (2 * x1) % 128 == 0 and x1 % tx == 0 and x2 % ROWS == 0
            and fine_block % (chunks * ROWS) == 0
        )
        if aligned:
            return aligned_device(tx, py, pz, chunks, fields, sources, green)
        return general_device(fields, sources, green)

    placed = (
        P("tx", None, "py", "pz", None),
        P("tx", None, "py", "pz", None),
        P(None, "pz", "py", None),
    )
    return jax.shard_map(
        on_device,
        mesh=mesh,
        in_specs=placed,
        out_specs=(P(None, "py", "pz", None), P("tx", None, "py", "pz", None)),
        check_vma=False,
    )
```

```python
import functools
import math

import jax
import jax.numpy as jnp
import ml_dtypes
import numpy as np
from jax import lax
from jax.experimental import pallas as pl
from jax.experimental.pallas import tpu as pltpu
from jax.sharding import PartitionSpec as P


F32 = jnp.float32
BF16 = jnp.bfloat16
NN = (((1,), (0,)), ((), ()))
NT = (((1,), (1,)), ((), ()))


def signed(count):
    index = np.arange(count)
    return np.where(index < count // 2, index, index - count)


def forward_matrix(coarse):
    index = np.arange(coarse)
    return np.exp(-2j * np.pi * ((index[:, None] * index[None, :]) % coarse) / coarse)


def inverse_matrix(coarse, fine):
    phases = (np.arange(fine)[:, None] * signed(coarse)[None, :]) % fine
    return np.exp(2j * np.pi * phases / fine) / coarse


def halves(matrix):
    high = matrix.astype(ml_dtypes.bfloat16)
    low = (matrix - high.astype(np.float64)).astype(ml_dtypes.bfloat16)
    return np.stack([high, low], axis=-3)


def block_form(matrix):
    re, im = matrix.real, matrix.imag
    return np.stack([np.stack([re, -im], 1), np.stack([im, re], 1)], 0)


def split(x):
    high = x.astype(BF16)
    return high, (x - high.astype(F32)).astype(BF16)


def product_left(m_ref, x, dims):
    high, low = split(x)
    mh, ml = m_ref[0], m_ref[1]
    dot = functools.partial(lax.dot_general, dimension_numbers=dims, preferred_element_type=F32)
    return dot(mh, high) + dot(mh, low) + dot(ml, high)


def product_right(x, m_ref):
    high, low = split(x)
    mh, ml = m_ref[0], m_ref[1]
    dot = functools.partial(lax.dot_general, dimension_numbers=NN, preferred_element_type=F32)
    return dot(high, mh) + dot(low, mh) + dot(high, ml)


def times_i(x):
    half = x.shape[1] // 2
    return jnp.concatenate([-x[:, half:], x[:, :half]], axis=1)


def depth_forward(m_ref, x_ref, o_ref):
    parts, _, rows, _ = o_ref.shape
    for s in range(x_ref.shape[3]):
        re, im = x_ref[0, 0, :, s, :], x_ref[0, 1, :, s, :]
        both = jnp.concatenate(
            [jnp.concatenate([re, -im], axis=1), jnp.concatenate([im, re], axis=1)], axis=0
        )
        out = product_left(m_ref, both, NT)
        for p in range(parts):
            o_ref[p, s] = out[p * rows : (p + 1) * rows]


def middle_forward(m_ref, x_ref, *o_refs):
    _, rows, lanes = o_refs[0].shape
    for s in range(x_ref.shape[2]):
        x = x_ref[:, :, s, :].reshape(-1, lanes)
        out = product_left(m_ref, jnp.concatenate([x, times_i(x)], axis=0), NN)
        for p, o_ref in enumerate(o_refs):
            o_ref[s] = out[p * rows : (p + 1) * rows]


def top_forward(parts, me_ref, m_ref, g_ref, *refs):
    x_refs, o_refs = refs[:parts], refs[parts:]
    count, rows, lanes = x_refs[0].shape
    x = jnp.concatenate([r[...].reshape(count * rows, lanes) for r in x_refs], axis=1)
    v = product_right(x, m_ref)
    coarse = v.shape[1] // 2
    vr, vi = v[:, :coarse], v[:, coarse:]
    gr, gi = g_ref[0].reshape(count * rows, coarse), g_ref[1].reshape(count * rows, coarse)
    wr = vr * gr - vi * gi
    wi = vr * gi + vi * gr
    wide = coarse // parts
    blocks = [
        jnp.concatenate([w[:, p * wide : (p + 1) * wide] for w in (wr, wi)], axis=1)
        for p in range(parts)
    ]
    me = me_ref[0]
    for j, o_ref in enumerate(o_refs):
        picked = blocks[0]
        for p in range(1, parts):
            picked = jnp.where((me ^ j) == p, blocks[p], picked)
        o_ref[...] = picked.reshape(count, rows, lanes)


def middle_inverse(slots, m_ref, *refs):
    x_refs, o_refs = refs[:slots], refs[slots:]
    parts, _, rows, _ = o_refs[0].shape
    for s in range(x_refs[0].shape[0]):
        x = jnp.concatenate([r[s] for r in x_refs], axis=0)
        out = product_left(m_ref, jnp.concatenate([x, times_i(x)], axis=0), NN)
        for p in range(parts):
            for h, o_ref in enumerate(o_refs):
                at = (p * len(o_refs) + h) * rows
                o_ref[p, s] = out[at : at + rows]


def middle_refine(m_ref, x_ref, o_ref):
    rows = o_ref.shape[2]
    for i in range(x_ref.shape[2]):
        pieces = [x_ref[q, c, i] for q in range(x_ref.shape[0]) for c in range(2)]
        out = product_left(m_ref, jnp.concatenate(pieces, axis=0), NN)
        o_ref[0, i] = out[:rows]
        o_ref[1, i] = out[rows:]


def last_product(t, m_ref):
    top = t.shape[0] // 2
    out = product_right(jnp.concatenate([t[:top], t[top:]], axis=1), m_ref)
    fine = out.shape[1] // 2
    return out[:, :fine], out[:, fine:]


def contrast_last(m1_ref, m3_ref, *refs):
    *x_refs, o_ref = refs
    lanes = x_refs[0].shape[3]
    for s in range(o_ref.shape[2]):
        x = jnp.concatenate([r[:, :, s, :].reshape(-1, lanes) for r in x_refs], axis=0)
        re, im = last_product(product_left(m1_ref, x, NN), m3_ref)
        o_ref[0, :, s, :] = re
        o_ref[1, :, s, :] = im


def scatter_last(slots, m1_ref, m3_ref, c_ref, *refs):
    x_refs, o_ref = refs[:slots], refs[-1]
    lanes = x_refs[0].shape[3]
    for s in range(o_ref.shape[3]):
        x = jnp.concatenate([r[:, :, s, :].reshape(-1, lanes) for r in x_refs], axis=1)
        re, im = last_product(product_left(m1_ref, x, NT), m3_ref)
        cr, ci = c_ref[0, :, s, :], c_ref[1, :, s, :]
        o_ref[0, 0, :, s, :] = cr * re - ci * im
        o_ref[0, 1, :, s, :] = cr * im + ci * re


def whole(array):
    zeros = (0,) * array.ndim
    return pl.BlockSpec(array.shape, lambda i: zeros)


def along(shape, axis, block, offset=0):
    sizes = tuple(block if a == axis else n for a, n in enumerate(shape))
    return pl.BlockSpec(sizes, lambda i: tuple(i + offset if a == axis else 0 for a in range(len(shape))))


def call(body, steps, in_specs, operands, shapes, out_specs, flops, aliases=None):
    moved = sum(math.prod(s.shape) * 4 for s in shapes) * 2
    return pl.pallas_call(
        body,
        grid=(steps,),
        in_specs=in_specs,
        out_specs=out_specs,
        out_shape=shapes,
        input_output_aliases=aliases or {},
        cost_estimate=pl.CostEstimate(flops=flops, bytes_accessed=moved, transcendentals=0),
        compiler_params=pltpu.CompilerParams(vmem_limit_bytes=56 * 2**20),
    )(*operands)


ROWS = 8


def shape_of(*dims):
    return jax.ShapeDtypeStruct(dims, F32)


def exchange(x, axis):
    return lax.all_to_all(x, axis, 0, 0, tiled=True)


def swap(x, axis, size, bit):
    return lax.ppermute(x, axis, [(i, i ^ bit) for i in range(size)])


def gather_slots(pieces, axis, size):
    bit = size // 2
    order = [(0, p) for p in pieces]
    while bit:
        order = order + [(j | bit, swap(p, axis, size, bit)) for j, p in order]
        bit //= 2
    return order


def aligned_device(tx, py, pz, chunks, fields, sources, green):
    coarse = fields.shape[4]
    fine = 2 * coarse
    x1, x2 = fields.shape[2], fields.shape[3]
    f1, f2 = fine // py, fine // pz
    lanes = 2 * x1
    part = x1 // tx
    k3 = coarse // pz
    me_y, me_z, me_x = lax.axis_index("py"), lax.axis_index("pz"), lax.axis_index("tx")

    fwd, inv = forward_matrix(coarse), inverse_matrix(coarse, fine)
    refine = inv @ fwd
    ri = lambda m: np.concatenate([m.real, m.imag], axis=1)
    m_fwd = jnp.asarray(halves(ri(fwd)))
    order = [[y ^ j for j in range(py)] for y in range(py)]
    rows2 = fwd.reshape(py, x1, coarse)
    m_mid_fwd = jnp.asarray(
        halves(np.stack([ri(rows2[o].reshape(coarse, coarse)) for o in order]))
    )[me_y]
    cols2 = inv.reshape(fine, py, x1)
    m_mid_inv = jnp.asarray(
        halves(np.stack([ri(cols2[:, o].reshape(fine, coarse)) for o in order]))
    )[me_y]
    top = block_form(fwd).reshape(2 * coarse, 2, py, x1).transpose(2, 1, 3, 0)
    m_top = jnp.asarray(
        halves(np.stack([top[o].reshape(2 * coarse, 2 * coarse) for o in order]))
    )[me_y]
    last = block_form(inv).transpose(2, 3, 0, 1).reshape(2 * coarse, 2 * fine)
    m_last = jnp.asarray(halves(last))
    last_c = block_form(refine).transpose(2, 3, 0, 1).reshape(2 * coarse, 2 * fine)
    m_last_c = jnp.asarray(halves(last_c))
    first = block_form(inv).reshape(2, py, f1, 2, py, x1)
    m_first = jnp.asarray(
        halves(
            np.stack(
                [
                    first[:, y][:, :, :, [y ^ j for j in range(py)]].transpose(0, 1, 3, 2, 4)
                    .reshape(2 * f1, 2 * coarse)
                    for y in range(py)
                ]
            )
        )
    )[me_y]
    mid = block_form(refine).reshape(2, pz, f2, 2, pz, x2).transpose(1, 0, 2, 4, 3, 5)
    m_mid = jnp.asarray(halves(mid.reshape(pz, 2 * f2, 2 * coarse)))[me_z]

    spec = call(
        depth_forward, x2 // ROWS,
        [whole(m_fwd), pl.BlockSpec((1, 2, x1, ROWS, coarse), lambda i: (0, 0, 0, i, 0))],
        (m_fwd, sources), [shape_of(pz, x2, k3, lanes)],
        [along((pz, x2, k3, lanes), 1, ROWS)],
        6 * 2 * x2 * coarse * coarse * lanes,
    )[0]
    spec = exchange(spec, "pz")

    fr, fi, sr, si = fields[:, 0], fields[:, 1], sources[:, 0], sources[:, 1]
    numer_re = jnp.sum(sr * fr + si * fi, axis=0)
    numer_im = jnp.sum(si * fr - sr * fi, axis=0)
    denom = jnp.sum(fr * fr + fi * fi, axis=0)
    sums = jnp.stack([numer_re, numer_im, denom])
    blocks = [lax.dynamic_slice_in_dim(sums, (me_x ^ j) * part, part, axis=1) for j in range(tx)]
    blocks = [blocks[0]] + [swap(blocks[j], "tx", tx, j) for j in range(1, tx)]
    total = functools.reduce(jnp.add, blocks)
    contrast = total[:2] / total[2:]
    spread = jnp.broadcast_to(contrast[None], (pz,) + contrast.shape)
    seen = exchange(spread, "pz")

    slab = (k3, x1, lanes)
    specs = call(
        middle_forward, k3 // ROWS,
        [whole(m_mid_fwd), along(spec.shape, 2, ROWS)],
        (m_mid_fwd, spec), [shape_of(*slab)] * py, [along(slab, 0, ROWS)] * py,
        6 * 2 * k3 * coarse * coarse * lanes,
    )
    specs = [specs[0]] + [swap(specs[j], "py", py, j) for j in range(1, py)]
    specs = call(
        functools.partial(top_forward, py), k3 // ROWS,
        [pl.BlockSpec(memory_space=pltpu.SMEM), whole(m_top), along(green.shape, 1, ROWS)]
        + [along(slab, 0, ROWS)] * py,
        (me_y.reshape(1), m_top, green, *specs),
        [shape_of(*slab)] * py, [along(slab, 0, ROWS)] * py,
        6 * 4 * k3 * x1 * coarse * coarse,
    )
    specs = [specs[0]] + [swap(specs[j], "py", py, j) for j in range(1, py)]

    some = f2 // chunks
    dims = (pz, k3, some, lanes)
    pieces = call(
        functools.partial(middle_inverse, py), k3 // ROWS,
        [whole(m_mid_inv)] + [along(slab, 0, ROWS)] * py,
        (m_mid_inv, *specs), [shape_of(*dims)] * chunks, [along(dims, 1, ROWS)] * chunks,
        6 * 2 * k3 * fine * coarse * lanes,
    )

    ref_dims = (2, part, f2, coarse)
    step = min(4, part)
    mine = call(
        middle_refine, part // step,
        [whole(m_mid), along(seen.shape, 2, step)],
        (m_mid, seen), [shape_of(*ref_dims)], [along(ref_dims, 1, step)],
        6 * 4 * part * f2 * coarse * coarse,
    )[0]
    slots = gather_slots([mine], "py", py)
    parts = [p for _, p in slots]
    bit, codes = tx // 2, [(j, 0) for j, _ in slots]
    while bit:
        parts = parts + [swap(p, "tx", tx, bit) for p in parts]
        codes = codes + [(j, t | bit) for j, t in codes]
        bit //= 2
    dim1 = block_form(refine).reshape(2, py, f1, 2, py, tx, part)
    table = np.stack(
        [
            np.stack(
                [dim1[:, y][:, :, :, y ^ j, t ^ k] for j, k in codes], axis=2
            ).reshape(2 * f1, 2 * coarse)
            for y in range(py)
            for t in range(tx)
        ]
    )
    m_first_c = jnp.asarray(halves(table))[me_y * tx + me_x]
    out_dims = (2, f1, f2, fine)
    contrast_fine = call(
        contrast_last, f2 // ROWS,
        [whole(m_first_c), whole(m_last_c)] + [along(ref_dims, 2, ROWS)] * len(parts),
        (m_first_c, m_last_c, *parts), [shape_of(*out_dims)], [along(out_dims, 2, ROWS)],
        6 * 8 * f1 * f2 * coarse * fine,
    )[0]

    scattered = None
    scat_dims = (1,) + out_dims
    for h, piece in enumerate(pieces):
        piece = exchange(piece, "pz")
        arrived = [p for _, p in gather_slots([piece], "py", py)]
        offset = h * some // ROWS
        specs = [whole(m_first), whole(m_last), along(out_dims, 2, ROWS, offset)]
        specs += [along(dims, 2, ROWS)] * py
        operands = (m_first, m_last, contrast_fine, *arrived)
        aliases = None
        if scattered is not None:
            aliases = {len(operands): 0}
            specs += [pl.BlockSpec(memory_space=pl.ANY)]
            operands += (scattered,)
        scattered = call(
            functools.partial(scatter_last, py), some // ROWS, specs, operands,
            [shape_of(*scat_dims)], [along(scat_dims, 3, ROWS, offset)],
            6 * 8 * f1 * some * coarse * fine, aliases,
        )[0]
    return contrast_fine, scattered


def fourier_matrix(out_index, in_index, period, exponent_sign, weight):
    phases = out_index[:, None] * in_index[None, :] % period
    angles = exponent_sign * 2.0 * math.pi / period * phases.astype(jnp.float32)
    cosine = weight * jnp.cos(angles)
    sine_part = weight * jnp.sin(angles)
    return jnp.stack([jnp.stack([cosine, -sine_part], 1), jnp.stack([sine_part, cosine], 1)], 0)


def local_step(values, matrix):
    return jnp.einsum("fcxyl,dkcl->fdyxk", values, matrix, precision=lax.Precision.HIGHEST)


def remote_step(values, matrix):
    return jnp.einsum("fclxy,dkcl->fdxyk", values, matrix, precision=lax.Precision.HIGHEST)


def turn(values, matrix, axis):
    return remote_step(lax.all_to_all(values, axis, split_axis=4, concat_axis=2, tiled=True), matrix)


def forward_pass(values, matrix):
    return turn(turn(local_step(values, matrix), matrix, "pz"), matrix, "py")


def inverse_pass(values, matrix):
    return turn(turn(local_step(values, matrix), matrix, "py"), matrix, "pz")


def complex_product(first_factor, second_factor):
    real_part = first_factor[0] * second_factor[0] - first_factor[1] * second_factor[1]
    imag_part = first_factor[0] * second_factor[1] + first_factor[1] * second_factor[0]
    return jnp.stack([real_part, imag_part])


def general_device(fields, sources, green):
    coarse = fields.shape[4]
    fine = 2 * coarse
    index = jnp.arange(coarse, dtype=jnp.int32)
    fine_index = jnp.arange(fine, dtype=jnp.int32)
    signed_coarse = jnp.where(index < coarse // 2, index, index - coarse)
    unit_coarse = jnp.ones((coarse, 1), F32)
    unit_fine = jnp.ones((fine, 1), F32)
    coarse_forward = fourier_matrix(index, index, coarse, -1.0, unit_coarse)
    padded_inverse = fourier_matrix(fine_index, signed_coarse, fine, 1.0, unit_fine / coarse)
    fr, fi, sr, si = fields[:, 0], fields[:, 1], sources[:, 0], sources[:, 1]
    numer_re = jnp.sum(sr * fr + si * fi, axis=0)
    numer_im = jnp.sum(si * fr - sr * fi, axis=0)
    denom = jnp.sum(fr * fr + fi * fi, axis=0)
    numer_re, numer_im, denom = lax.psum((numer_re, numer_im, denom), "tx")
    contrast = jnp.stack([numer_re / denom, numer_im / denom])[None]
    contrast_fine = inverse_pass(forward_pass(contrast, coarse_forward), padded_inverse)[0]
    spectrum = forward_pass(sources[0:1], coarse_forward)
    weighted = complex_product(spectrum[0], green)[None]
    domain_field = inverse_pass(weighted, padded_inverse)[0]
    return contrast_fine, complex_product(contrast_fine, domain_field)[None]


def power_of_two(n):
    return n & (n - 1) == 0


def solution(mesh):
    tx, py, pz = mesh.shape["tx"], mesh.shape["py"], mesh.shape["pz"]
    chunks = 4

    def on_device(fields, sources, green):
        x1, x2, coarse = fields.shape[2:]
        fine_block = 2 * coarse // pz
        aligned = (
            power_of_two(tx) and power_of_two(py) and coarse % 128 == 0
            and (2 * x1) % 128 == 0 and x1 % tx == 0 and x2 % ROWS == 0
            and fine_block % (chunks * ROWS) == 0
        )
        if aligned:
            return aligned_device(tx, py, pz, chunks, fields, sources, green)
        return general_device(fields, sources, green)

    placed = (
        P("tx", None, "py", "pz", None),
        P("tx", None, "py", "pz", None),
        P(None, "pz", "py", None),
    )
    return jax.shard_map(
        on_device,
        mesh=mesh,
        in_specs=placed,
        out_specs=(P(None, "py", "pz", None), P("tx", None, "py", "pz", None)),
        check_vma=False,
    )
```
